32 devices in a mesh: field: 16 (over z, y, core), probe: 2 (over x).
Axes of the slice: x: 2, y: 2, z: 4, core: 2. Of those that a mesh axis runs over, the one named last changes fastest.
Arguments:
- probes: bfloat16 [16, 4, 512, 256], P('probe', None, 'field'), may hold values from -6 to 6
- matern_shift: float32 [4, 512, 256], P(None, 'field'), may hold values from 0.25 to 2
- diffusivity: float32 [4, 512, 256], P(None, 'field'), may hold values from 0.03 to 0.1
- sensor_count: int32 [16], P('field'), may hold values from 1 to 256, 2560 in all
- sensor_cell: int32 [16, 256], P('field'), may hold values from 0 to 32767
- sensor_owner: int32 [16, 256, 1], P('field'), may hold values from 0 to 15; in each aligned block of 256 rows (0 to 255, 256 to 511, ..., all dimensions but the last counted through in order) at most 24 rows name the same one
- design_logit: float32 [16, 16, 24], P('field'), may hold values from -6 to 6
- noise_precision: float32 [16, 16, 24], P('field'), may hold values from 1 to 8
Outputs:
- hessian_probes: float32 [16, 4, 512, 256], P('probe', None, 'field')
- tiles: float32 [16, 16], P('probe')
- weight_grad: float32 [16, 16, 24], P('field')
The draws below stay inside these ranges and needn't reach their ends.
Inputs may be any that keep to these rules, and one draw needn't show every extreme that they name: `sensor_count`: the counts sum to 2560 and the largest is 256. `sensor_cell`: flat cell index within the block; several slots may share a cell. `sensor_owner`: among the 256 slots of one block, live or not, no owner is named by more than 24 slots, a bound that some block reaches.
All inputs are finite; a program needn't handle non-finite values. No bound on the sum of `sensor_count` on one device may be relied on, other than what follows from the above.
Results may differ from the reference program's by a relative error of at most 0.00035.
Values may be sent and summed in bfloat16 or wider, within the bound.
A program may use at most 128 MiB of HBM per device.

```python
import math
import jax
import jax.numpy as jnp
import numpy as np
from jax import lax

NZ = 4
CX = 32
NY = 256
SMAX = 256
SWEEPS = 4
STEPS = 6
SENSORS = 2560
CAP = 24
PROBES = 16
NX = 512
CELLS = 32768
N_FIELD = 16


def set_ends(drawn, rng, low, high):
    shape = drawn.shape
    index_at = [jax.random.randint(jax.random.fold_in(rng, axis), (), 0, shape[axis]) for axis in range(len(shape))]
    drawn = drawn.at[tuple(index_at)].set(low)
    longest = shape.index(max(shape))
    index_at[longest] = (index_at[longest] + 1) % shape[longest]
    return drawn.at[tuple(index_at)].set(high)


def block_levels(key, dims, pieces, low, top_value):
    factor_of, own = 1.0, jax.random.fold_in(key, 6)
    for dim, blocks in pieces:
        draws = jnp.exp(jax.random.uniform(jax.random.fold_in(own, dim), (blocks,), jnp.float32, low / len(pieces), top_value / len(pieces)))
        factor_of = factor_of * jnp.repeat(draws, dims[dim] // blocks).reshape([-1 if axis == dim else 1 for axis in range(len(dims))])
    return factor_of


def split_up(amount, total, bound, skew):
    weights = [(1 << 20) // math.isqrt(rank ** skew) + 1 for rank in range(2, amount + 1)]
    surplus, counts = total - bound - (amount - 1), [1] * (amount - 1)
    while surplus > 0:
        candidates = [i for i in range(amount - 1) if counts[i] < bound]
        mass, left = sum([weights[i] for i in candidates]), surplus
        for i in candidates:
            extra = min(bound - counts[i], max(1, left * weights[i] // mass), surplus)
            counts[i] = counts[i] + extra
            surplus = surplus - extra
    return np.array([bound] + counts)


def ragged_sizes(rng, count, total, limit, skew):
    if count == 2:
        one = jax.random.randint(rng, (), max(1, total - limit), min(limit, total - 1) + 1)
        return jnp.stack([one, total - one])
    lengths = jnp.asarray(split_up(count, total, limit, skew), jnp.int32)
    twos = (count - 1) // 2
    source_of, sink = lengths[1:1 + 2 * twos:2], lengths[2:2 + 2 * twos:2]
    slack = jnp.minimum(source_of - 1, limit - sink)
    shifted = jax.random.randint(jax.random.fold_in(rng, 1), (twos,), 0, 1 << 20) % (slack + 1)
    lengths = lengths.at[1:1 + 2 * twos:2].set(source_of - shifted).at[2:2 + 2 * twos:2].set(sink + shifted)
    return lengths[jax.random.permutation(jax.random.fold_in(rng, 2), count)]


def assign_block(key, own, number, rows, amount, top, limit, slope):
    order = jax.random.permutation(key, amount)
    heavy_load, ordinary = load_shares(amount, rows * top, limit, slope, True), load_shares(amount, rows * top, limit, slope, False)
    places = jnp.arange(amount)

    def named(tallies, turn):
        used = int((tallies > 0).sum())
        fixed = max(1, used // 4)
        shifted = fixed + (places - fixed + turn * (used - fixed)) % max(1, amount - fixed)
        return jnp.zeros((amount,), jnp.int32).at[order[jnp.where(places < fixed, places, shifted)]].set(jnp.asarray(tallies, jnp.int32))

    tallies = jnp.where(number % 4 == 0, named(heavy_load, number // 4), named(ordinary, number - number // 4 - 1))
    mixed = jax.random.permutation(jax.random.fold_in(own, 3), amount)
    donor, receiver = mixed[0:amount // 2 * 2:2], mixed[1:amount // 2 * 2:2]
    slack = jnp.minimum(tallies[donor] - 1, limit - tallies[receiver]) // 2
    slack = jnp.where((donor == order[0]) | (receiver == order[0]) | (tallies[receiver] == 0), 0, jnp.maximum(slack, 0))
    shifted = jax.random.randint(jax.random.fold_in(own, 4), (amount // 2,), 0, 1 << 20) % (slack + 1)
    tallies = tallies.at[donor].add(-shifted).at[receiver].add(shifted)
    items = jnp.searchsorted(jnp.cumsum(tallies), jnp.arange(rows * top), side="right").astype(jnp.int32)
    table = items.reshape(top, rows).T
    table = table[jax.random.permutation(jax.random.fold_in(own, 1), rows)]
    turn = jax.random.randint(jax.random.fold_in(own, 2), (rows, 1), 0, top)
    return jnp.take_along_axis(table, (jnp.arange(top)[None, :] + turn) % top, axis=1)


def load_shares(count, total, limit, lean, full):
    loads = [(1 << 20) // math.isqrt(standing ** lean) + 1 for standing in range(1, count + 1)]
    largest = limit if full else min(limit, max(-(-total // count), total * loads[0] // sum(loads)))
    least = 1 if total - largest >= count - 1 else 0
    holding, spare = [largest] + [least] * (count - 1), total - largest - least * (count - 1)
    while spare > 0:
        free = [i for i in range(1, count) if holding[i] < largest] or [i for i in range(1, count) if holding[i] < limit]
        mass, left = sum([loads[i] for i in free]), spare
        for i in free:
            extra = min(limit - holding[i], max(1, left * loads[i] // mass), spare)
            holding[i] = holding[i] + extra
            spare = spare - extra
    return np.array(holding)


def bell_draw(stream_key, shape, scale, bound, pieces=(), kind=jnp.bfloat16):
    entries = scale * jax.random.normal(stream_key, shape, jnp.float32)
    if pieces:
        entries = entries * block_levels(stream_key, shape, pieces, -0.22, 0.18)
    return jnp.clip(entries, -bound, bound).astype(kind)


def setup_inputs(seed: int = 0) -> dict:
    keys = jax.random.split(jax.random.key(seed), 9)
    probes = bell_draw(keys[0], (PROBES, NZ, NX, NY), 1.0, 6.0, ((0, 2), (2, 16)))
    matern_shift = jnp.clip(jnp.exp(math.log(2.0) - 2.0794415 * jax.random.uniform(keys[1], (NZ, NX, NY), jnp.float32) ** block_levels(keys[1], (NZ, NX, NY), ((1, 16),), -0.2, 0.2)), 0.25, 2.0)
    diffusivity = jnp.clip(jnp.exp(math.log(0.1) - 1.2039728 * jax.random.uniform(keys[2], (NZ, NX, NY), jnp.float32) ** block_levels(keys[2], (NZ, NX, NY), ((1, 16),), -0.2, 0.2)), 0.03, 0.1)
    sensor_count = ragged_sizes(keys[3], N_FIELD, SENSORS, SMAX, 2).astype(jnp.int32)
    sensor_cell = set_ends(jax.random.randint(keys[4], (N_FIELD, SMAX), 0, CELLS), jax.random.fold_in(keys[4], 1), 0, CELLS - 1).astype(jnp.int32)
    sensor_owner_keys = jax.random.split(jax.random.fold_in(keys[5], 1), N_FIELD * SMAX // SMAX)
    sensor_owner_turns = jax.random.permutation(jax.random.fold_in(keys[5], 3), N_FIELD * SMAX // SMAX)
    sensor_owner = jax.vmap(lambda own, number: assign_block(jax.random.fold_in(keys[5], 2), own, number, SMAX, N_FIELD, 1, CAP, 2))(sensor_owner_keys, sensor_owner_turns).reshape((N_FIELD, SMAX, 1))
    design_logit = bell_draw(keys[6], (N_FIELD, N_FIELD, CAP), 1.5, 6.0, ((0, 16),), jnp.float32)
    noise_precision = jnp.clip(jnp.exp(math.log(8.0) - 2.0794415 * jax.random.uniform(keys[7], (N_FIELD, N_FIELD, CAP), jnp.float32) ** block_levels(keys[7], (N_FIELD, N_FIELD, CAP), ((0, 16),), -0.2, 0.2)), 1.0, 8.0)
    return dict(probes=probes, matern_shift=matern_shift, diffusivity=diffusivity, sensor_count=sensor_count, sensor_cell=sensor_cell, sensor_owner=sensor_owner, design_logit=design_logit, noise_precision=noise_precision)


advect_speed = 0.3

def neighbours(field):
    west_cells = jnp.roll(field, 1, axis=1)
    east_cells = jnp.roll(field, -1, axis=1)
    side_pad = jnp.pad(field, ((0, 0), (0, 0), (1, 1)))
    depth_pad = jnp.pad(field, ((1, 1), (0, 0), (0, 0)))
    beside_all = west_cells + east_cells + (side_pad[:, :, :-2] + side_pad[:, :, 2:]) + (depth_pad[:-2] + depth_pad[2:])
    return (beside_all, west_cells, east_cells)

def prior_apply(source, diagonal):
    state = source / diagonal
    for sweep in range(SWEEPS):
        beside_all, west_cells, east_cells = neighbours(state)
        state = (source + beside_all) / diagonal
    return state

def forward_apply(state, diffusivity):
    for sweep in range(STEPS):
        beside_all, west_cells, east_cells = neighbours(state)
        state = state + diffusivity * (beside_all - 6.0 * state) - advect_speed * (state - west_cells)
    return state

def adjoint_apply(state, diffusivity):
    for sweep in range(STEPS):
        scaled = diffusivity * state
        beside_all, west_cells, east_cells = neighbours(scaled)
        east_state = jnp.roll(state, -1, axis=1)
        state = state + (beside_all - 6.0 * scaled) - advect_speed * (state - east_state)
    return state

def to_blocks(field):
    return field.reshape(NZ, N_FIELD, CX, NY).transpose(1, 0, 2, 3).reshape(N_FIELD, CELLS)

def from_blocks(blocks):
    return blocks.reshape(N_FIELD, NZ, CX, NY).transpose(1, 0, 2, 3).reshape(NZ, NX, NY)

def reference(probes, matern_shift, diffusivity, sensor_count, sensor_cell, sensor_owner, design_logit, noise_precision):
    diagonal = matern_shift + 6.0
    slots = jnp.arange(SMAX, dtype=jnp.int32)
    live = (slots[None, :] < sensor_count[:, None]).astype(jnp.float32)
    owner = sensor_owner[:, :, 0]
    same = owner[:, :, None] == owner[:, None, :]
    earlier = slots[None, :] < slots[:, None]
    position = lax.optimization_barrier(jnp.sum(jnp.logical_and(same, earlier[None]), axis=2)).astype(jnp.int32)
    source = jnp.broadcast_to(jnp.arange(N_FIELD, dtype=jnp.int32)[:, None], (N_FIELD, SMAX))
    gated = jax.nn.sigmoid(design_logit[owner, source, position])
    weight_slot = gated * noise_precision[owner, source, position]

    def one_probe(sumsq, probe):
        field = probe.astype(jnp.float32)
        state = forward_apply(prior_apply(field, diagonal), diffusivity)
        observed = jnp.take_along_axis(to_blocks(state), sensor_cell, axis=1) * live
        returned = observed * weight_slot
        injected = jnp.zeros((N_FIELD, CELLS), jnp.float32).at[source, sensor_cell].add(returned)
        result = prior_apply(adjoint_apply(from_blocks(injected), diffusivity), diagonal)
        return (sumsq + observed * observed, result)
    sumsq, hessian_probes = lax.scan(one_probe, jnp.zeros((N_FIELD, SMAX), jnp.float32), probes)
    squares = jnp.zeros((N_FIELD, N_FIELD, CAP), jnp.float32).at[owner, source, position].add(sumsq)
    all_gate = jax.nn.sigmoid(design_logit)
    weight_grad = all_gate * (1.0 - all_gate) * noise_precision * squares
    flat_result = hessian_probes.reshape(PROBES, -1)
    flat_probe = probes.reshape(PROBES, -1).astype(jnp.float32)
    tiles = jnp.dot(flat_result, flat_probe.T, precision=lax.Precision.HIGHEST) * (1.0 / math.sqrt(SENSORS))
    return (hessian_probes, tiles, weight_grad)
```

```python
import functools
import math

import jax
import jax.numpy as jnp
from jax import lax
from jax.experimental import pallas as pl
from jax.experimental.pallas import tpu as pltpu
from jax.sharding import PartitionSpec as P

SWEEPS = 4
STEPS = 6
HALO = SWEEPS + STEPS
SENS_DEV = 160
ADVECT = 0.3
LANES = 128
F32 = jnp.float32
HIGHEST = lax.Precision.HIGHEST


def rows_of(ref, row, per):
    block = ref[pl.ds(row * per, per)]
    return [block[i].astype(F32) for i in range(per)]


def put_rows(ref, row, per, values):
    for i in range(per):
        ref[row * per + i] = values[i]


def around(west, mid, east, halves, at_first, at_last):
    per = len(mid)
    zero = jnp.zeros_like(mid[0])
    fwd = [pltpu.roll(t, 1, 1) for t in mid]
    bwd = [pltpu.roll(t, LANES - 1, 1) for t in mid]
    out = []
    for i in range(per):
        half = i % halves
        prev = fwd[i - 1] if half > 0 else zero
        following = bwd[i + 1] if half < halves - 1 else zero
        side = jnp.where(at_first, prev, fwd[i]) + jnp.where(at_last, following, bwd[i])
        total = (west[i] + east[i]) + side
        depth = [mid[j] for j in (i - halves, i + halves) if 0 <= j < per]
        if len(depth) == 2:
            total = total + (depth[0] + depth[1])
        elif depth:
            total = total + depth[0]
        out.append(total)
    return out


def kernel(
    dims,
    p_in,
    c_in,
    cell_s,
    count_s,
    cell_v,
    owner_v,
    logit,
    noise,
    h_out,
    t_out,
    g_out,
    src,
    coef,
    kap,
    rec,
    buf_a,
    buf_b,
    inj,
    wpad,
    wsend,
    wrecv,
    wfield,
    obs,
    msend,
    mrecv,
    sq2d,
    local_sem,
    halo_send,
    halo_recv,
    w_send,
    w_recv,
    o_send,
    o_recv,
    m_send,
    m_recv,
):
    nf, npr, nz, cx, ny, cap, slots = dims
    halves = ny // LANES
    per = nz * halves
    wide = cx + 2 * HALO
    end = HALO + cx
    me = lax.axis_index("field")
    mine = lax.axis_index("probe")
    left = lax.rem(me + nf - 1, nf)
    right = lax.rem(me + 1, nf)

    own_p = pltpu.make_async_copy(p_in, src.at[pl.ds(HALO * per, cx * per)], local_sem.at[0])
    own_c = pltpu.make_async_copy(c_in, coef.at[pl.ds(HALO, cx)], local_sem.at[1])
    own_p.start()
    own_c.start()

    barrier = pltpu.get_barrier_semaphore()
    for j in range(1, nf):
        pl.semaphore_signal(
            barrier,
            inc=1,
            device_id={"field": lax.rem(me + j, nf)},
            device_id_type=pl.DeviceIdType.MESH,
        )
    for j in range(1, npr):
        pl.semaphore_signal(
            barrier,
            inc=1,
            device_id={"probe": lax.rem(mine + j, npr)},
            device_id_type=pl.DeviceIdType.MESH,
        )
    pl.semaphore_wait(barrier, nf + npr - 2)

    def send(source, target, send_sem, recv_sem, where):
        return pltpu.make_async_remote_copy(
            src_ref=source,
            dst_ref=target,
            send_sem=send_sem,
            recv_sem=recv_sem,
            device_id=where,
            device_id_type=pl.DeviceIdType.MESH,
        )

    def halo_pair(source, source_row, target, scale, first):
        to_right = send(
            source.at[pl.ds((source_row + cx - HALO) * scale, HALO * scale)],
            target.at[pl.ds(0, HALO * scale)],
            halo_send.at[first],
            halo_recv.at[first],
            {"field": right},
        )
        to_left = send(
            source.at[pl.ds(source_row * scale, HALO * scale)],
            target.at[pl.ds(end * scale, HALO * scale)],
            halo_send.at[first + 1],
            halo_recv.at[first + 1],
            {"field": left},
        )
        to_right.start()
        to_left.start()
        return [to_right, to_left]

    edge_c = halo_pair(c_in, 0, coef, 1, 0)
    edge_p = halo_pair(p_in, 0, src, per, 2)

    gated = jax.nn.sigmoid(logit[...])
    wpad[...] = jnp.zeros_like(wpad)
    wpad[:, :cap] = gated * noise[...]
    for b in range(nf):
        wsend[b] = jnp.broadcast_to(wpad[b : b + 1, :], (8, LANES))
    wrecv[me] = wsend[me]
    w_copies = []
    for j in range(1, nf):
        other = lax.rem(me + j, nf)
        copy = send(
            wsend.at[other], wrecv.at[me], w_send.at[j - 1], w_recv.at[j - 1], {"field": other}
        )
        copy.start()
        w_copies.append(copy)

    sub = lax.broadcasted_iota(jnp.int32, (slots, slots), 0)
    lan = lax.broadcasted_iota(jnp.int32, (slots, slots), 1)
    eye = sub == lan

    def column(row):
        return jnp.sum(jnp.where(eye, row, 0.0), axis=1, keepdims=True)

    cell = cell_v[...]
    shift_x = ny.bit_length() - 1
    shift_z = shift_x + cx.bit_length() - 1
    line_row = ((cell >> shift_x) & (cx - 1)) * nz + (cell >> shift_z)
    owner_row = owner_v[...].astype(F32)
    y_col = column((cell & (ny - 1)).astype(F32))
    owner_col = column(owner_row)
    pos_col = jnp.sum(
        jnp.where(jnp.logical_and(owner_col == owner_row, lan < sub), 1.0, 0.0),
        axis=1,
        keepdims=True,
    )
    count = count_s[0]
    lane_pos = lax.broadcasted_iota(jnp.int32, (slots, LANES), 1).astype(F32)
    pos_hot = lane_pos == pos_col

    own_c.wait()
    own_p.wait()

    def spread(x, carry):
        tile = coef[x]
        for z in range(nz):
            for h in range(halves):
                at = slice(h * LANES, (h + 1) * LANES)
                kap[x * per + z * halves + h] = jnp.broadcast_to(tile[z : z + 1, at], (8, LANES))
                rec[x * per + z * halves + h] = 1.0 / jnp.broadcast_to(
                    tile[nz + z : nz + z + 1, at] + 6.0, (8, LANES)
                )
        return carry

    lax.fori_loop(HALO, end, spread, 0)
    for copy in edge_c:
        copy.wait()
    lax.fori_loop(0, HALO, spread, 0)
    lax.fori_loop(end, wide, spread, 0)

    lane = lax.broadcasted_iota(jnp.int32, (8, LANES), 1)
    at_first = lane == 0
    at_last = lane == LANES - 1
    ring = functools.partial(around, halves=halves, at_first=at_first, at_last=at_last)
    span = range(per)

    def prior(origin, out_first, out_last, buffers):
        def start(row):
            s = rows_of(origin, row, per)
            r = rows_of(rec, row, per)
            return [s[i] * r[i] for i in span]

        reach = SWEEPS
        for sweep in range(SWEEPS):
            reach -= 1
            first, last = out_first - reach, out_last + reach
            target, target_row = buffers[sweep + 1]
            if sweep == 0:
                load = start
            else:
                load = functools.partial(rows_of, buffers[sweep][0], per=per)

            def body(x, carry, load=load, target=target, target_row=target_row):
                west, mid = carry[:per], carry[per:]
                east = load(x + 1)
                ring_sum = ring(west, mid, east)
                s = rows_of(origin, x, per)
                r = rows_of(rec, x, per)
                put_rows(target, x - target_row, per, [(s[i] + ring_sum[i]) * r[i] for i in span])
                return tuple(mid) + tuple(east)

            lax.fori_loop(
                first, last, body, tuple(load(first - 1)) + tuple(load(first)), unroll=2
            )

    for copy in edge_p:
        copy.wait()
    flip = ((None, 0), (buf_a, 0), (buf_b, 0), (buf_a, 0), (buf_b, 0))
    prior(src, HALO - STEPS, end + STEPS, flip)

    for step in range(STEPS):
        u, new = (buf_b, buf_a) if step % 2 == 0 else (buf_a, buf_b)
        reach = STEPS - 1 - step

        def body(x, carry, u=u, new=new):
            west, mid = carry[:per], carry[per:]
            east = rows_of(u, x + 1, per)
            ring_sum = ring(west, mid, east)
            k = rows_of(kap, x, per)
            put_rows(
                new,
                x,
                per,
                [
                    k[i] * ring_sum[i]
                    + ((1.0 - ADVECT) - 6.0 * k[i]) * mid[i]
                    + ADVECT * west[i]
                    for i in span
                ],
            )
            return tuple(mid) + tuple(east)

        first, last = HALO - reach, end + reach
        lax.fori_loop(
            first,
            last,
            body,
            tuple(rows_of(u, first - 1, per)) + tuple(rows_of(u, first, per)),
            unroll=2,
        )
    state = buf_b if STEPS % 2 == 0 else buf_a
    spare = buf_a if STEPS % 2 == 0 else buf_b

    for copy in w_copies:
        copy.wait()
    chosen = jnp.zeros((slots, LANES), F32)
    for o in range(nf):
        chosen = jnp.where(owner_col == float(o), wrecv[o][0:1, :], chosen)
    live_col = lax.broadcasted_iota(jnp.int32, (slots, 1), 0) < count
    weight_col = jnp.sum(jnp.where(pos_hot, chosen, 0.0), axis=1, keepdims=True)
    weight_col = jnp.where(live_col, weight_col, 0.0)
    line_iota = lax.broadcasted_iota(jnp.int32, (cx * nz, slots), 0)
    line_hot = jnp.where(line_iota == line_row, 1.0, 0.0)
    lane_y = lax.broadcasted_iota(jnp.int32, (slots, ny), 1).astype(F32)
    y_weight = jnp.where(lane_y == y_col, weight_col, 0.0)
    wfield[...] = jnp.dot(line_hot, y_weight, precision=HIGHEST, preferred_element_type=F32)
    weight_row = jnp.sum(jnp.where(eye, weight_col, 0.0), axis=0, keepdims=True)

    group = 8 // nz

    def inject(g, carry):
        tile = wfield[pl.ds(pl.multiple_of(g * 8, 8), 8), :]
        for r in range(8):
            for h in range(halves):
                at = (HALO + g * group + r // nz) * per + (r % nz) * halves + h
                w = jnp.broadcast_to(tile[r : r + 1, h * LANES : (h + 1) * LANES], (8, LANES))
                inj[at] = state[at] * w
        return carry

    lax.fori_loop(0, cx // group, inject, 0)
    edge_v = halo_pair(inj, HALO, inj, per, 4)

    for part in range(slots // LANES):

        def pick(s, held, part=part):
            c = cell_s[0, part * LANES + s]
            y = c & (ny - 1)
            at = (HALO + ((c >> shift_x) & (cx - 1))) * per
            at = at + (c >> shift_z) * halves + (y >> 7)
            turn = (s - y) & (LANES - 1)
            return jnp.where(lane == s, pltpu.roll(state[at], turn, 1), held)

        held = lax.fori_loop(0, LANES, pick, jnp.zeros((8, LANES), F32), unroll=8)
        held = jnp.where(lane + part * LANES < count, held, 0.0)
        obs[mine, :, part * LANES : (part + 1) * LANES] = held
    o_copies = []
    for j in range(1, npr):
        other = lax.rem(mine + j, npr)
        copy = send(
            obs.at[mine], obs.at[mine], o_send.at[j - 1], o_recv.at[j - 1], {"probe": other}
        )
        copy.start()
        o_copies.append(copy)

    for copy in edge_v:
        copy.wait()

    def adjoint_steps(lo, hi, v):
        for step in range(lo, hi):
            new = spare if step % 2 == 0 else state

            def body(x, carry, v=v, new=new):
                q_west, q_mid, mid = carry[:per], carry[per : 2 * per], carry[2 * per :]
                east = rows_of(v, x + 1, per)
                k = rows_of(kap, x + 1, per)
                q_east = [k[i] * east[i] for i in span]
                ring_sum = ring(q_west, q_mid, q_east)
                put_rows(
                    new,
                    x,
                    per,
                    [
                        (ring_sum[i] - 6.0 * q_mid[i])
                        + ((1.0 - ADVECT) * mid[i] + ADVECT * east[i])
                        for i in span
                    ],
                )
                return tuple(q_mid) + tuple(q_east) + tuple(east)

            first, last = step + 1, wide - step - 1
            v0, v1 = rows_of(v, first - 1, per), rows_of(v, first, per)
            k0, k1 = rows_of(kap, first - 1, per), rows_of(kap, first, per)
            q0 = [k0[i] * v0[i] for i in span]
            q1 = [k1[i] * v1[i] for i in span]
            lax.fori_loop(first, last, body, tuple(q0) + tuple(q1) + tuple(v1), unroll=2)
            v = new
        return v

    v = adjoint_steps(0, 4, inj)

    for copy in o_copies:
        copy.wait()
    weighted = obs[mine] * weight_row
    squares = jnp.zeros((1, slots), F32)
    msend[:, 0] = jnp.zeros((nf, 8, LANES), F32)
    for q in range(npr):
        seen = obs[q]
        squares = squares + jnp.sum(seen * seen, axis=0, keepdims=True)
        tile = lax.dot_general(
            weighted, seen, (((1,), (1,)), ((), ())), precision=HIGHEST, preferred_element_type=F32
        )
        for f in range(nf):
            msend[f, 0, :, q * 8 : q * 8 + 8] = tile
    owner_iota = lax.broadcasted_iota(jnp.int32, (nf, slots), 0).astype(F32)
    owner_squares = jnp.where(owner_iota == owner_row, squares, 0.0)
    by_owner = jnp.dot(
        owner_squares,
        jnp.where(pos_hot, 1.0, 0.0),
        precision=HIGHEST,
        preferred_element_type=F32,
    )
    for o in range(nf):
        msend[o, 1] = jnp.broadcast_to(by_owner[o : o + 1, :], (8, LANES))
    mrecv[me] = msend[me]
    m_copies = []
    for j in range(1, nf):
        other = lax.rem(me + j, nf)
        copy = send(
            msend.at[other], mrecv.at[me], m_send.at[j - 1], m_recv.at[j - 1], {"field": other}
        )
        copy.start()
        m_copies.append(copy)

    v = adjoint_steps(4, STEPS, v)
    free = spare if v is state else state
    prior(v, HALO, end, ((None, 0), (free, 0), (inj, 0), (free, 0), (h_out, HALO)))

    for copy in m_copies:
        copy.wait()
    total = mrecv[0, 0]
    for f in range(1, nf):
        total = total + mrecv[f, 0]
    t_out[...] = total[:, : npr * 8] * (1.0 / math.sqrt(SENS_DEV * nf))
    for f in range(nf):
        sq2d[f : f + 1, :] = mrecv[f, 1][0:1, :]
    gate = jax.nn.sigmoid(logit[...])
    g_out[...] = gate * (1.0 - gate) * noise[...] * sq2d[:, :cap]


def on_device(
    probes,
    matern_shift,
    diffusivity,
    sensor_count,
    sensor_cell,
    sensor_owner,
    design_logit,
    noise_precision,
):
    nf, npr = lax.axis_size("field"), lax.axis_size("probe")
    count, nz, cx, ny = probes.shape
    cap, slots = design_logit.shape[2], sensor_cell.shape[1]
    halves = ny // LANES
    per = nz * halves
    wide = cx + 2 * HALO
    tiles_in = (
        probes.reshape(count, nz, cx, halves, LANES)
        .transpose(2, 1, 3, 0, 4)
        .reshape(cx * per, count, LANES)
    )
    coef_in = jnp.concatenate([diffusivity, matern_shift], axis=0).transpose(1, 0, 2)
    dims = (nf, npr, nz, cx, ny, cap, slots)
    vmem = pl.BlockSpec(memory_space=pltpu.VMEM)
    smem = pl.BlockSpec(memory_space=pltpu.SMEM)
    anywhere = pl.BlockSpec(memory_space=pl.ANY)
    dma = pltpu.SemaphoreType.DMA
    tall = pltpu.VMEM((wide * per, count, LANES), F32)
    hess, tiles, grad = pl.pallas_call(
        functools.partial(kernel, dims),
        out_shape=(
            jax.ShapeDtypeStruct((cx * per, count, LANES), F32),
            jax.ShapeDtypeStruct((count, npr * count), F32),
            jax.ShapeDtypeStruct((nf, cap), F32),
        ),
        in_specs=[anywhere, anywhere, smem, smem, vmem, vmem, vmem, vmem],
        out_specs=(vmem, vmem, vmem),
        scratch_shapes=[
            pltpu.VMEM((wide * per, count, LANES), jnp.bfloat16),
            pltpu.VMEM((wide, 2 * nz, ny), F32),
            tall,
            tall,
            tall,
            tall,
            tall,
            pltpu.VMEM((nf, LANES), F32),
            pltpu.VMEM((nf, 8, LANES), F32),
            pltpu.VMEM((nf, 8, LANES), F32),
            pltpu.VMEM((cx * nz, ny), F32),
            pltpu.VMEM((npr, count, slots), F32),
            pltpu.VMEM((nf, 2, 8, LANES), F32),
            pltpu.VMEM((nf, 2, 8, LANES), F32),
            pltpu.VMEM((nf, LANES), F32),
            dma((2,)),
            dma((6,)),
            dma((6,)),
            dma((nf - 1,)),
            dma((nf - 1,)),
            dma((npr - 1,)),
            dma((npr - 1,)),
            dma((nf - 1,)),
            dma((nf - 1,)),
        ],
        compiler_params=pltpu.CompilerParams(collective_id=0, has_side_effects=True),
        name="hessian_pass",
    )(
        tiles_in,
        coef_in,
        sensor_cell,
        sensor_count,
        sensor_cell,
        sensor_owner[:, :, 0],
        design_logit[0],
        noise_precision[0],
    )
    hess = (
        hess.reshape(cx, nz, halves, count, LANES)
        .transpose(3, 1, 0, 2, 4)
        .reshape(count, nz, cx, ny)
    )
    return hess, tiles, grad[None]


def solution(mesh):
    in_specs = (
        P("probe", None, "field", None),
        P(None, "field", None),
        P(None, "field", None),
        P("field"),
        P("field", None),
        P("field", None, None),
        P("field", None, None),
        P("field", None, None),
    )
    out_specs = (P("probe", None, "field", None), P("probe", None), P("field", None, None))
    return jax.shard_map(
        on_device, mesh=mesh, in_specs=in_specs, out_specs=out_specs, check_vma=False
    )
```

```python
import functools
import math

import jax
import jax.numpy as jnp
from jax import lax
from jax.experimental import pallas as pl
from jax.experimental.pallas import tpu as pltpu
from jax.sharding import PartitionSpec as P

SWEEPS = 4
STEPS = 6
HALO = SWEEPS + STEPS
SENS_DEV = 160
ADVECT = 0.3
LANES = 128
F32 = jnp.float32
HIGHEST = lax.Precision.HIGHEST


def rows_of(ref, row, per):
    block = ref[pl.ds(row * per, per)]
    return [block[i].astype(F32) for i in range(per)]


def put_rows(ref, row, per, values):
    for i in range(per):
        ref[row * per + i] = values[i]


def around(west, mid, east, at_first, at_last):
    per = len(mid)
    out = []
    for i in range(per):
        other = mid[i ^ 1]
        if i % 2 == 0:
            far = jnp.where(at_first, 0.0, pltpu.roll(other, 1, 1))
        else:
            far = jnp.where(at_last, 0.0, pltpu.roll(other, LANES - 1, 1))
        total = (west[i] + east[i]) + (other + far)
        depth = [mid[j] for j in (i - 2, i + 2) if 0 <= j < per]
        if len(depth) == 2:
            total = total + (depth[0] + depth[1])
        elif depth:
            total = total + depth[0]
        out.append(total)
    return out


def reorder(value, matrix):
    out = None
    for piece in range(3):
        part = value.astype(jnp.bfloat16)
        term = jnp.dot(part, matrix, preferred_element_type=F32)
        out = term if out is None else out + term
        if piece < 2:
            value = value - part.astype(F32)
    return out


def kernel(
    dims,
    p_in,
    c_in,
    cell_s,
    count_s,
    cell_v,
    owner_v,
    logit,
    noise,
    h_out,
    t_out,
    g_out,
    raw,
    src,
    coef,
    kap,
    keep,
    rec,
    buf_a,
    buf_b,
    inj,
    wpad,
    wsend,
    wrecv,
    wfield,
    obs,
    msend,
    mrecv,
    sq2d,
    local_sem,
    halo_send,
    halo_recv,
    w_send,
    w_recv,
    o_send,
    o_recv,
    m_send,
    m_recv,
):
    nf, npr, nz, cx, ny, cap, slots = dims
    halves = ny // LANES
    per = nz * halves
    wide = cx + 2 * HALO
    end = HALO + cx
    me = lax.axis_index("field")
    mine = lax.axis_index("probe")
    left = lax.rem(me + nf - 1, nf)
    right = lax.rem(me + 1, nf)

    own_p = pltpu.make_async_copy(p_in, raw.at[pl.ds(HALO * nz, cx * nz)], local_sem.at[0])
    own_c = pltpu.make_async_copy(c_in, coef.at[pl.ds(HALO, cx)], local_sem.at[1])
    own_p.start()
    own_c.start()

    barrier = pltpu.get_barrier_semaphore()
    for j in range(1, nf):
        pl.semaphore_signal(
            barrier,
            inc=1,
            device_id={"field": lax.rem(me + j, nf)},
            device_id_type=pl.DeviceIdType.MESH,
        )
    for j in range(1, npr):
        pl.semaphore_signal(
            barrier,
            inc=1,
            device_id={"probe": lax.rem(mine + j, npr)},
            device_id_type=pl.DeviceIdType.MESH,
        )
    pl.semaphore_wait(barrier, nf + npr - 2)

    def send(source, target, send_sem, recv_sem, where):
        return pltpu.make_async_remote_copy(
            src_ref=source,
            dst_ref=target,
            send_sem=send_sem,
            recv_sem=recv_sem,
            device_id=where,
            device_id_type=pl.DeviceIdType.MESH,
        )

    def halo_pair(source, source_row, target, scale, first):
        to_right = send(
            source.at[pl.ds((source_row + cx - HALO) * scale, HALO * scale)],
            target.at[pl.ds(0, HALO * scale)],
            halo_send.at[first],
            halo_recv.at[first],
            {"field": right},
        )
        to_left = send(
            source.at[pl.ds(source_row * scale, HALO * scale)],
            target.at[pl.ds(end * scale, HALO * scale)],
            halo_send.at[first + 1],
            halo_recv.at[first + 1],
            {"field": left},
        )
        to_right.start()
        to_left.start()
        return [to_right, to_left]

    edge_c = halo_pair(c_in, 0, coef, 1, 0)
    edge_p = halo_pair(p_in, 0, raw, nz, 2)

    gated = jax.nn.sigmoid(logit[...])
    wpad[...] = jnp.zeros_like(wpad)
    wpad[:, :cap] = gated * noise[...]
    for b in range(nf):
        wsend[b] = jnp.broadcast_to(wpad[b : b + 1, :], (8, LANES))
    wrecv[me] = wsend[me]
    w_copies = []
    for j in range(1, nf):
        other = lax.rem(me + j, nf)
        copy = send(
            wsend.at[other], wrecv.at[me], w_send.at[j - 1], w_recv.at[j - 1], {"field": other}
        )
        copy.start()
        w_copies.append(copy)

    sub = lax.broadcasted_iota(jnp.int32, (slots, slots), 0)
    lan = lax.broadcasted_iota(jnp.int32, (slots, slots), 1)
    eye = sub == lan

    def column(row):
        return jnp.sum(jnp.where(eye, row, 0.0), axis=1, keepdims=True)

    cell = cell_v[...]
    shift_x = ny.bit_length() - 1
    shift_z = shift_x + cx.bit_length() - 1
    line_row = ((cell >> shift_x) & (cx - 1)) * nz + (cell >> shift_z)
    owner_row = owner_v[...].astype(F32)
    y_at = cell & (ny - 1)
    y_col = column(((y_at & 1) * LANES + (y_at >> 1)).astype(F32))
    owner_col = column(owner_row)
    pos_col = jnp.sum(
        jnp.where(jnp.logical_and(owner_col == owner_row, lan < sub), 1.0, 0.0),
        axis=1,
        keepdims=True,
    )
    count = count_s[0]
    lane_pos = lax.broadcasted_iota(jnp.int32, (slots, LANES), 1).astype(F32)
    pos_hot = lane_pos == pos_col

    ny_sub = lax.broadcasted_iota(jnp.int32, (ny, ny), 0)
    ny_lan = lax.broadcasted_iota(jnp.int32, (ny, ny), 1)
    split = jnp.where(ny_sub == 2 * (ny_lan & (LANES - 1)) + (ny_lan >> 7), 1.0, 0.0)
    split = split.astype(jnp.bfloat16)
    merge = jnp.where(ny_lan == 2 * (ny_sub & (LANES - 1)) + (ny_sub >> 7), 1.0, 0.0)
    merge = merge.astype(jnp.bfloat16)

    def sort_coef(first, count_x):
        value = coef[pl.ds(first, count_x)].reshape(count_x * 2 * nz, ny)
        coef[pl.ds(first, count_x)] = reorder(value, split).reshape(count_x, 2 * nz, ny)

    def sort_probes(first, count_x):
        value = raw[pl.ds(first * nz, count_x * nz)].astype(F32)
        value = value.reshape(count_x * nz * 8, ny).astype(jnp.bfloat16)
        value = jnp.dot(value, split, preferred_element_type=F32)
        for i in range(count_x * nz):
            for h in range(halves):
                src[(first * nz + i) * halves + h] = value[
                    i * 8 : i * 8 + 8, h * LANES : (h + 1) * LANES
                ]

    def spread(x, carry):
        tile = coef[x]
        for z in range(nz):
            for h in range(halves):
                at = slice(h * LANES, (h + 1) * LANES)
                row = x * per + z * halves + h
                k = jnp.broadcast_to(tile[z : z + 1, at], (8, LANES))
                kap[row] = k
                keep[row] = (1.0 - ADVECT) - 6.0 * k
                rec[row] = 1.0 / jnp.broadcast_to(tile[nz + z : nz + z + 1, at] + 6.0, (8, LANES))
        return carry

    own_c.wait()
    sort_coef(HALO, cx)
    lax.fori_loop(HALO, end, spread, 0, unroll=2)
    own_p.wait()
    sort_probes(HALO, cx)
    for copy in edge_c:
        copy.wait()
    sort_coef(0, HALO)
    sort_coef(end, HALO)
    lax.fori_loop(0, HALO, spread, 0, unroll=2)
    lax.fori_loop(end, wide, spread, 0, unroll=2)

    lane = lax.broadcasted_iota(jnp.int32, (8, LANES), 1)
    at_first = lane == 0
    at_last = lane == LANES - 1
    ring = functools.partial(around, at_first=at_first, at_last=at_last)
    span = range(per)

    def prior(origin, out_first, out_last, buffers):
        def start(row):
            s = rows_of(origin, row, per)
            r = rows_of(rec, row, per)
            return [s[i] * r[i] for i in span]

        reach = SWEEPS
        for sweep in range(SWEEPS):
            reach -= 1
            first, last = out_first - reach, out_last + reach
            target, target_row = buffers[sweep + 1]
            if sweep == 0:
                load = start
            else:
                load = functools.partial(rows_of, buffers[sweep][0], per=per)

            def body(x, carry, load=load, target=target, target_row=target_row):
                west, mid = carry[:per], carry[per:]
                east = load(x + 1)
                ring_sum = ring(west, mid, east)
                s = rows_of(origin, x, per)
                r = rows_of(rec, x, per)
                put_rows(target, x - target_row, per, [(s[i] + ring_sum[i]) * r[i] for i in span])
                return tuple(mid) + tuple(east)

            lax.fori_loop(
                first, last, body, tuple(load(first - 1)) + tuple(load(first)), unroll=2
            )

    for copy in edge_p:
        copy.wait()
    sort_probes(0, HALO)
    sort_probes(end, HALO)
    flip = ((None, 0), (buf_a, 0), (buf_b, 0), (buf_a, 0), (buf_b, 0))
    prior(src, HALO - STEPS, end + STEPS, flip)

    for step in range(STEPS):
        u, new = (buf_b, buf_a) if step % 2 == 0 else (buf_a, buf_b)
        reach = STEPS - 1 - step

        def body(x, carry, u=u, new=new):
            west = rows_of(u, x - 1, per)
            mid = rows_of(u, x, per)
            east = rows_of(u, x + 1, per)
            ring_sum = ring(west, mid, east)
            k = rows_of(kap, x, per)
            c = rows_of(keep, x, per)
            values = [k[i] * ring_sum[i] + (c[i] * mid[i] + ADVECT * west[i]) for i in span]
            put_rows(new, x, per, values)
            return carry

        lax.fori_loop(HALO - reach, end + reach, body, 0, unroll=2)
    state = buf_b if STEPS % 2 == 0 else buf_a
    spare = buf_a if STEPS % 2 == 0 else buf_b

    for copy in w_copies:
        copy.wait()
    chosen = jnp.zeros((slots, LANES), F32)
    for o in range(nf):
        chosen = jnp.where(owner_col == float(o), wrecv[o][0:1, :], chosen)
    live_col = lax.broadcasted_iota(jnp.int32, (slots, 1), 0) < count
    weight_col = jnp.sum(jnp.where(pos_hot, chosen, 0.0), axis=1, keepdims=True)
    weight_col = jnp.where(live_col, weight_col, 0.0)
    line_iota = lax.broadcasted_iota(jnp.int32, (cx * nz, slots), 0)
    line_hot = jnp.where(line_iota == line_row, 1.0, 0.0)
    lane_y = lax.broadcasted_iota(jnp.int32, (slots, ny), 1).astype(F32)
    y_weight = jnp.where(lane_y == y_col, weight_col, 0.0)
    wfield[...] = jnp.dot(line_hot, y_weight, precision=HIGHEST, preferred_element_type=F32)
    weight_row = jnp.sum(jnp.where(eye, weight_col, 0.0), axis=0, keepdims=True)

    group = 8 // nz

    def inject(g, carry):
        tile = wfield[pl.ds(pl.multiple_of(g * 8, 8), 8), :]
        for r in range(8):
            for h in range(halves):
                at = (HALO + g * group + r // nz) * per + (r % nz) * halves + h
                w = jnp.broadcast_to(tile[r : r + 1, h * LANES : (h + 1) * LANES], (8, LANES))
                inj[at] = state[at] * w
        return carry

    lax.fori_loop(0, cx // group, inject, 0)
    edge_v = halo_pair(inj, HALO, inj, per, 4)

    for part in range(slots // LANES):

        def pick(s, held, part=part):
            c = cell_s[0, part * LANES + s]
            y = c & (ny - 1)
            at = (HALO + ((c >> shift_x) & (cx - 1))) * per
            at = at + (c >> shift_z) * halves + (y & 1)
            turn = (s - (y >> 1)) & (LANES - 1)
            return jnp.where(lane == s, pltpu.roll(state[at], turn, 1), held)

        held = lax.fori_loop(0, LANES, pick, jnp.zeros((8, LANES), F32), unroll=8)
        held = jnp.where(lane + part * LANES < count, held, 0.0)
        obs[mine, :, part * LANES : (part + 1) * LANES] = held
    o_copies = []
    for j in range(1, npr):
        other = lax.rem(mine + j, npr)
        copy = send(
            obs.at[mine], obs.at[mine], o_send.at[j - 1], o_recv.at[j - 1], {"probe": other}
        )
        copy.start()
        o_copies.append(copy)

    for copy in edge_v:
        copy.wait()

    def adjoint_steps(lo, hi, v):
        for step in range(lo, hi):
            new = spare if step % 2 == 0 else state

            def body(x, carry, v=v, new=new):
                q_west, q_mid = carry[:per], carry[per:]
                mid = rows_of(v, x, per)
                east = rows_of(v, x + 1, per)
                k = rows_of(kap, x + 1, per)
                c = rows_of(keep, x, per)
                q_east = [k[i] * east[i] for i in span]
                ring_sum = ring(q_west, q_mid, q_east)
                values = [ring_sum[i] + (c[i] * mid[i] + ADVECT * east[i]) for i in span]
                put_rows(new, x, per, values)
                return tuple(q_mid) + tuple(q_east)

            first, last = step + 1, wide - step - 1
            v0, v1 = rows_of(v, first - 1, per), rows_of(v, first, per)
            k0, k1 = rows_of(kap, first - 1, per), rows_of(kap, first, per)
            q0 = [k0[i] * v0[i] for i in span]
            q1 = [k1[i] * v1[i] for i in span]
            lax.fori_loop(first, last, body, tuple(q0) + tuple(q1), unroll=2)
            v = new
        return v

    v = adjoint_steps(0, 4, inj)

    for copy in o_copies:
        copy.wait()
    weighted = obs[mine] * weight_row
    squares = jnp.zeros((1, slots), F32)
    msend[:, 0] = jnp.zeros((nf, 8, LANES), F32)
    for q in range(npr):
        seen = obs[q]
        squares = squares + jnp.sum(seen * seen, axis=0, keepdims=True)
        tile = lax.dot_general(
            weighted, seen, (((1,), (1,)), ((), ())), precision=HIGHEST, preferred_element_type=F32
        )
        for f in range(nf):
            msend[f, 0, :, q * 8 : q * 8 + 8] = tile
    owner_iota = lax.broadcasted_iota(jnp.int32, (nf, slots), 0).astype(F32)
    owner_squares = jnp.where(owner_iota == owner_row, squares, 0.0)
    by_owner = jnp.dot(
        owner_squares,
        jnp.where(pos_hot, 1.0, 0.0),
        precision=HIGHEST,
        preferred_element_type=F32,
    )
    for o in range(nf):
        msend[o, 1] = jnp.broadcast_to(by_owner[o : o + 1, :], (8, LANES))
    mrecv[me] = msend[me]
    m_copies = []
    for j in range(1, nf):
        other = lax.rem(me + j, nf)
        copy = send(
            msend.at[other], mrecv.at[me], m_send.at[j - 1], m_recv.at[j - 1], {"field": other}
        )
        copy.start()
        m_copies.append(copy)

    v = adjoint_steps(4, STEPS, v)
    free = spare if v is state else state
    prior(v, HALO, end, ((None, 0), (free, 0), (inj, 0), (free, 0), (inj, 0)))

    chunk = cx // 4
    for first in range(0, cx, chunk):
        tiles = inj[pl.ds((HALO + first) * per, chunk * per)]
        tiles = tiles.reshape(chunk * nz, halves, 8, LANES)
        sides = [tiles[:, h].reshape(chunk * nz * 8, LANES) for h in range(halves)]
        value = reorder(jnp.concatenate(sides, axis=1), merge)
        h_out[pl.ds(first * nz, chunk * nz)] = value.reshape(chunk * nz, 8, ny)


    for copy in m_copies:
        copy.wait()
    total = mrecv[0, 0]
    for f in range(1, nf):
        total = total + mrecv[f, 0]
    t_out[...] = total[:, : npr * 8] * (1.0 / math.sqrt(SENS_DEV * nf))
    for f in range(nf):
        sq2d[f : f + 1, :] = mrecv[f, 1][0:1, :]
    gate = jax.nn.sigmoid(logit[...])
    g_out[...] = gate * (1.0 - gate) * noise[...] * sq2d[:, :cap]


def on_device(
    probes,
    matern_shift,
    diffusivity,
    sensor_count,
    sensor_cell,
    sensor_owner,
    design_logit,
    noise_precision,
):
    nf, npr = lax.axis_size("field"), lax.axis_size("probe")
    count, nz, cx, ny = probes.shape
    cap, slots = design_logit.shape[2], sensor_cell.shape[1]
    halves = ny // LANES
    per = nz * halves
    wide = cx + 2 * HALO
    tiles_in = probes.transpose(2, 1, 0, 3).reshape(cx * nz, count, ny)
    coef_in = jnp.concatenate([diffusivity, matern_shift], axis=0).transpose(1, 0, 2)
    dims = (nf, npr, nz, cx, ny, cap, slots)
    vmem = pl.BlockSpec(memory_space=pltpu.VMEM)
    smem = pl.BlockSpec(memory_space=pltpu.SMEM)
    anywhere = pl.BlockSpec(memory_space=pl.ANY)
    dma = pltpu.SemaphoreType.DMA
    tall = pltpu.VMEM((wide * per, count, LANES), F32)
    hess, tiles, grad = pl.pallas_call(
        functools.partial(kernel, dims),
        out_shape=(
            jax.ShapeDtypeStruct((cx * nz, count, ny), F32),
            jax.ShapeDtypeStruct((count, npr * count), F32),
            jax.ShapeDtypeStruct((nf, cap), F32),
        ),
        in_specs=[anywhere, anywhere, smem, smem, vmem, vmem, vmem, vmem],
        out_specs=(vmem, vmem, vmem),
        scratch_shapes=[
            pltpu.VMEM((wide * nz, count, ny), jnp.bfloat16),
            tall,
            pltpu.VMEM((wide, 2 * nz, ny), F32),
            tall,
            tall,
            tall,
            tall,
            tall,
            tall,
            pltpu.VMEM((nf, LANES), F32),
            pltpu.VMEM((nf, 8, LANES), F32),
            pltpu.VMEM((nf, 8, LANES), F32),
            pltpu.VMEM((cx * nz, ny), F32),
            pltpu.VMEM((npr, count, slots), F32),
            pltpu.VMEM((nf, 2, 8, LANES), F32),
            pltpu.VMEM((nf, 2, 8, LANES), F32),
            pltpu.VMEM((nf, LANES), F32),
            dma((2,)),
            dma((6,)),
            dma((6,)),
            dma((nf - 1,)),
            dma((nf - 1,)),
            dma((npr - 1,)),
            dma((npr - 1,)),
            dma((nf - 1,)),
            dma((nf - 1,)),
        ],
        compiler_params=pltpu.CompilerParams(collective_id=0, has_side_effects=True),
        name="hessian_pass",
    )(
        tiles_in,
        coef_in,
        sensor_cell,
        sensor_count,
        sensor_cell,
        sensor_owner[:, :, 0],
        design_logit[0],
        noise_precision[0],
    )
    hess = hess.reshape(cx, nz, count, ny).transpose(2, 1, 0, 3)
    return hess, tiles, grad[None]


def solution(mesh):
    in_specs = (
        P("probe", None, "field", None),
        P(None, "field", None),
        P(None, "field", None),
        P("field"),
        P("field", None),
        P("field", None, None),
        P("field", None, None),
        P("field", None, None),
    )
    out_specs = (P("probe", None, "field", None), P("probe", None), P("field", None, None))
    return jax.shard_map(
        on_device, mesh=mesh, in_specs=in_specs, out_specs=out_specs, check_vma=False
    )
```
